32 devices in a mesh: pipe: 4 (over z), tensor: 4 (over x, core), dp: 2 (over y).
Axes of the slice: x: 2, y: 2, z: 4, core: 2. Of those that a mesh axis runs over, the one named last changes fastest.
Arguments:
- inputs: bfloat16 [2, 128, 4096], P(None, ('tensor', 'dp')), may hold values from -6 to 6
- weights: bfloat16 [2, 4, 4096, 4096], P(None, 'pipe', None, 'tensor'), may hold values from -0.09375 to 0.09375
- norm_gains: float32 [2, 4, 4096], P(None, 'pipe'), may hold values from 0.1 to 1.9
- cotangent: bfloat16 [2, 128, 4096], P(None, ('tensor', 'dp')), may hold values from -6 to 6
Outputs:
- act_factor: bfloat16 [4096, 2, 4, 4096], P(('tensor', 'dp'), None, 'pipe')
- grad_factor: bfloat16 [4096, 2, 4, 4096], P(('tensor', 'dp'), None, 'pipe')
The draws below stay inside these ranges and needn't reach their ends.
All inputs are finite; a program needn't handle non-finite values.
Results may differ from the reference program's by a relative error of at most 0.025.
Values may be sent and summed in bfloat16 or wider, within the bound.
A program may use at most 192 MiB of HBM per device.

```python
import jax
import jax.numpy as jnp
from jax import lax

D = 4096
MB_DEV = 16
MICRO = 2
SLOTS = 2
LAYERS = 8
MICRO_TOKENS = 128
N_PIPE = 4
N_TENSOR = 4
N_DP = 2


def steps_of(own_key, dims, split, least, largest):
    def one(dim, parts):
        draws = jax.random.uniform(jax.random.fold_in(jax.random.fold_in(own_key, 6), dim), (parts,), jnp.float32, least / len(split), largest / len(split))
        return jnp.repeat(jnp.exp(draws), dims[dim] // parts).reshape((-1,) + (1,) * (len(dims) - dim - 1))

    loudness = one(*split[0])
    for cut in split[1:]:
        loudness = loudness * one(*cut)
    return loudness


def gaussian(key, shape, deviation, bound, split=(), dtype=jnp.bfloat16):
    array = deviation * jax.random.normal(key, shape, jnp.float32)
    if split:
        array = array * steps_of(key, shape, split, -0.22, 0.18)
    return jnp.clip(array, -bound, bound).astype(dtype)


def setup_inputs(seed: int = 0) -> dict:
    key_of = jax.random.split(jax.random.key(seed), 5)
    inputs = gaussian(key_of[0], (MICRO, MICRO_TOKENS, D), 1.0, 6.0, ((1, 8),))
    weights = gaussian(key_of[1], (SLOTS, N_PIPE, D, D), D ** -0.5, 0.09375, ((1, 4), (3, 4)))
    norm_gains = jnp.clip(1.0 + 0.18 * jax.random.normal(key_of[2], (SLOTS, N_PIPE, D), jnp.float32), 0.1, 1.9)
    cotangent = gaussian(key_of[3], (MICRO, MICRO_TOKENS, D), 1.0, 6.0, ((1, 8),))
    return {"inputs": inputs, "weights": weights, "norm_gains": norm_gains, "cotangent": cotangent}


EPSILON = 1e-05

def normalize(hidden, gain_row):
    hidden_wide = hidden.astype(jnp.float32)
    inverse_rms = lax.rsqrt(lax.optimization_barrier(jnp.mean(hidden_wide * hidden_wide, axis=-1, keepdims=True)) + EPSILON)
    normed = (hidden_wide * inverse_rms * gain_row).astype(jnp.bfloat16)
    return (hidden_wide, inverse_rms, normed)

def rounded(values):
    return lax.optimization_barrier(values.astype(jnp.bfloat16)).astype(jnp.float32)

def group_gram(tokens):
    grouped = tokens.reshape(MICRO, N_TENSOR, N_DP, MB_DEV, D)

    def add_group(group_pick, totals):
        chosen = lax.dynamic_index_in_dim(grouped, group_pick, 2, keepdims=False)
        flat_rows = chosen.reshape(MICRO * N_TENSOR * MB_DEV, D)
        gram = lax.dot_general(flat_rows, flat_rows, (((0,), (0,)), ((), ())), preferred_element_type=jnp.float32)
        return totals + rounded(gram * (1.0 / (MICRO * MICRO_TOKENS)))
    totals = lax.fori_loop(0, N_DP, add_group, jnp.zeros((D, D), jnp.float32))
    return totals.astype(jnp.bfloat16)

def reference(inputs, weights, norm_gains, cotangent):
    quarter = D // N_TENSOR
    hidden = inputs
    saved_hidden = []
    act_list = []
    for layer_index in range(LAYERS):
        slot_pick = layer_index // N_PIPE
        section_pick = layer_index % N_PIPE
        hidden_wide, inverse_rms, normed = normalize(hidden, norm_gains[slot_pick, section_pick])
        saved_hidden.append(hidden)
        act_list.append(group_gram(normed))
        if layer_index + 1 < LAYERS:
            product = jnp.dot(normed.reshape(-1, D), weights[slot_pick, section_pick], preferred_element_type=jnp.float32)
            product = product.astype(jnp.bfloat16).reshape(hidden.shape)
            hidden = (hidden_wide + product.astype(jnp.float32)).astype(jnp.bfloat16)
    delta = cotangent
    grad_list = [None] * LAYERS
    for layer_index in reversed(range(LAYERS)):
        grad_list[layer_index] = group_gram(delta)
        if layer_index > 0:
            slot_pick = layer_index // N_PIPE
            section_pick = layer_index % N_PIPE
            weight = weights[slot_pick, section_pick]
            gain_row = norm_gains[slot_pick, section_pick]
            flat_delta = delta.reshape(-1, D)
            back_sum = jnp.zeros(flat_delta.shape, jnp.float32)
            for column in range(N_TENSOR):
                lower = column * quarter
                upper = lower + quarter
                term = lax.dot_general(flat_delta[:, lower:upper], weight[:, lower:upper], (((1,), (1,)), ((), ())), preferred_element_type=jnp.float32)
                back_sum = back_sum + rounded(term)
            back_sum = back_sum.reshape(delta.shape)
            hidden_wide, inverse_rms, normed = normalize(saved_hidden[layer_index], gain_row)
            scaled = gain_row * back_sum
            inner = lax.optimization_barrier(jnp.mean(hidden_wide * scaled, axis=-1, keepdims=True))
            delta = (delta.astype(jnp.float32) + inverse_rms * scaled - inverse_rms ** 3 * hidden_wide * inner).astype(jnp.bfloat16)
    act_factor = jnp.stack(act_list, 0).reshape(SLOTS, N_PIPE, D, D).transpose(2, 0, 1, 3)
    grad_factor = jnp.stack(grad_list, 0).reshape(SLOTS, N_PIPE, D, D).transpose(2, 0, 1, 3)
    return (act_factor, grad_factor)
```

```python
import functools

import jax
import jax.numpy as jnp
from jax import lax
from jax.experimental import pallas as pl
from jax.experimental.pallas import tpu as pltpu
from jax.sharding import PartitionSpec as P

EPSILON = 1e-05


def peer_of(c, k):
    return lax.rem(c // 2 + k // 2, 2) * 2 + lax.rem(c + k, 2)


def chain_kernel(
    dims,
    x_ref,
    w_hbm,
    g_ref,
    cot_ref,
    h_out,
    d_out,
    w,
    hbuf,
    dbuf,
    acc,
    nxt,
    psend,
    rbuf,
    dnext,
    w_sem,
    own_sem,
    in_send,
    in_recv,
    f1_send,
    f1_recv,
    fx_send,
    fx_recv,
    b1_send,
    b1_recv,
    bx_send,
    bx_recv,
    rs_send,
    rs_recv,
    dp_send,
    dp_recv,
    loc_sem,
):
    micro, slots, rows, width, quarter, pipes, tensors, dps = dims
    items = slots * micro
    layers = slots * pipes
    group = tensors * rows
    p = lax.axis_index("pipe")
    c = lax.axis_index("tensor")
    d = lax.axis_index("dp")
    after = lax.rem(p + 1, pipes)
    before = lax.rem(p + pipes - 1, pipes)

    def where(pp, cc, dd):
        return {"pipe": pp, "tensor": cc, "dp": dd}

    def remote(src, dst, send, recv, target):
        return pltpu.make_async_remote_copy(
            src_ref=src,
            dst_ref=dst,
            send_sem=send,
            recv_sem=recv,
            device_id=target,
            device_id_type=pl.DeviceIdType.MESH,
        )

    w_copies = [
        pltpu.make_async_copy(w_hbm.at[s, 0], w.at[s], w_sem.at[s]) for s in range(slots)
    ]
    for copy in w_copies:
        copy.start()

    barrier = pltpu.get_barrier_semaphore()
    partners = [where(p, peer_of(c, k), d) for k in range(1, tensors)]
    partners += [where(after, c, d), where(before, c, d)]
    partners += [where(p, c, lax.rem(d + k, dps)) for k in range(1, dps)]
    for partner in partners:
        pl.semaphore_signal(
            barrier, inc=1, device_id=partner, device_id_type=pl.DeviceIdType.MESH
        )
    pl.semaphore_wait(barrier, len(partners))

    def row_ds(cc):
        return pl.ds(pl.multiple_of(cc * rows, rows), rows)

    def col_ds(cc):
        return pl.ds(pl.multiple_of(cc * quarter, quarter), quarter)

    def opening(src, buf, m, k):
        return remote(
            src.at[m],
            buf.at[m, row_ds(c)],
            in_send.at[m, k - 1],
            in_recv.at[m, k - 1],
            where(p, peer_of(c, k), d),
        )

    def opening_all(src, buf):
        for m in range(micro):
            for k in range(1, tensors):
                opening(src, buf, m, k).start()
        for m in range(micro):
            pltpu.make_async_copy(src.at[m], buf.at[m, row_ds(c)], own_sem.at[m]).start()

    def opening_wait(src, buf, m):
        pltpu.make_async_copy(src.at[m], buf.at[m, row_ds(c)], own_sem.at[m]).wait()
        for k in range(1, tensors):
            opening(src, buf, m, k).wait_recv()

    @pl.when(p == 0)
    def _():
        opening_all(x_ref, hbuf)

    @pl.when(p == pipes - 1)
    def _():
        opening_all(cot_ref, dbuf)

    def to_dp(buf, out, item, slot, m, which, k):
        return remote(
            buf.at[item],
            out.at[slot, d, m],
            dp_send.at[which, item, k - 1],
            dp_recv.at[which, item, k - 1],
            where(p, c, lax.rem(d + k, dps)),
        )

    def to_own(buf, out, item, slot, m, which):
        return pltpu.make_async_copy(
            buf.at[item], out.at[slot, d, m], loc_sem.at[which, item]
        )

    def f_slice(item, cc):
        return hbuf.at[item, :, col_ds(cc)]

    def f_along(item, target_item):
        return remote(
            nxt.at[item],
            f_slice(target_item, c),
            f1_send.at[item],
            f1_recv.at[target_item],
            where(after, c, d),
        )

    def spread(make_slice, item, part, send, recv):
        owner = peer_of(c, 2) if part == 2 else c
        target = peer_of(c, 2) if part == 1 else peer_of(c, 1)
        ref = make_slice(item, owner)
        return remote(ref, ref, send.at[item, part], recv.at[item, part], where(p, target, d))

    def f_step(item, carry):
        slot = item // micro
        m = lax.rem(item, micro)
        layer = slot * pipes + p
        target_item = item + micro * ((p + 1) // pipes)

        @pl.when(m == 0)
        def _():
            pltpu.make_async_copy(w_hbm.at[slot, 0], w.at[slot], w_sem.at[slot]).wait()

        fx = functools.partial(spread, f_slice, item, send=fx_send, recv=fx_recv)

        @pl.when(layer == 0)
        def _():
            opening_wait(x_ref, hbuf, item)

        @pl.when(layer > 0)
        def _():
            f_along(item, item).wait_recv()
            fx(part=1).start()
            fx(part=0).start()

        def piece(cc, first):
            part = hbuf[item, :, col_ds(cc)].astype(jnp.float32)
            scaled = (part * g_ref[slot, :, col_ds(cc)]).astype(jnp.bfloat16)
            product = jnp.dot(scaled, w[slot, col_ds(cc), :], preferred_element_type=jnp.float32)
            if first:
                acc[...] = product
            else:
                acc[...] += product
            return jnp.sum(part * part, axis=-1, keepdims=True)

        total = piece(c, True)

        @pl.when(layer > 0)
        def _():
            fx(part=0).wait_recv()

        total += piece(peer_of(c, 1), False)

        @pl.when(layer > 0)
        def _():
            fx(part=1).wait_recv()
            fx(part=2).start()

        total += piece(peer_of(c, 2), False)

        @pl.when(layer > 0)
        def _():
            fx(part=2).wait_recv()

        total += piece(peer_of(c, 3), False)

        @pl.when(layer < layers - 1)
        def _():
            inverse_rms = lax.rsqrt(total * (1.0 / width) + EPSILON)
            product = (acc[...] * inverse_rms).astype(jnp.bfloat16).astype(jnp.float32)
            nxt[item] = (hbuf[item, :, col_ds(c)].astype(jnp.float32) + product).astype(
                jnp.bfloat16
            )
            f_along(item, target_item).start()

        to_own(hbuf, h_out, item, slot, m, 0).start()
        for k in range(1, dps):
            to_dp(hbuf, h_out, item, slot, m, 0, k).start()
        return carry

    lax.fori_loop(0, items, f_step, 0)

    def b_slice(item, cc):
        return dbuf.at[item, row_ds(cc)]

    def b_along(item, target_item):
        return remote(
            dnext.at[item],
            b_slice(target_item, c),
            b1_send.at[item],
            b1_recv.at[target_item],
            where(before, c, d),
        )

    blocks = width // quarter

    def reduce_copy(item, k, n):
        return remote(
            psend.at[item, row_ds(peer_of(c, k)), pl.ds(n * quarter, quarter)],
            rbuf.at[item, k - 1, :, pl.ds(n * quarter, quarter)],
            rs_send.at[item, k - 1, n],
            rs_recv.at[item, k - 1, n],
            where(p, peer_of(c, k), d),
        )

    def b_step(item, carry):
        slot = slots - 1 - item // micro
        m = lax.rem(item, micro)
        layer = slot * pipes + p
        target_item = item + micro * (1 - (p + pipes - 1) // pipes)
        bx = functools.partial(spread, b_slice, item, send=bx_send, recv=bx_recv)

        @pl.when(layer == layers - 1)
        def _():
            opening_wait(cot_ref, dbuf, item)

        @pl.when(layer < layers - 1)
        def _():
            b_along(item, item).wait_recv()
            bx(part=1).start()
            bx(part=0).start()
            bx(part=1).wait_recv()
            bx(part=2).start()
            bx(part=0).wait_recv()
            bx(part=2).wait_recv()

        @pl.when(layer > 0)
        def _():
            columns = dbuf[item, :, col_ds(c)]
            for n in range(blocks):
                psend[item, :, n * quarter : (n + 1) * quarter] = lax.dot_general(
                    columns,
                    w[slot, n * quarter : (n + 1) * quarter, :],
                    (((1,), (1,)), ((), ())),
                    preferred_element_type=jnp.float32,
                ).astype(jnp.bfloat16)
                for k in range(tensors - 1, 0, -1):
                    reduce_copy(item, k, n).start()

        to_own(dbuf, d_out, item, slot, m, 1).start()
        for k in range(1, dps):
            to_dp(dbuf, d_out, item, slot, m, 1, k).start()

        @pl.when(layer > 0)
        def _():
            for n in range(blocks):
                for k in range(1, tensors):
                    reduce_copy(item, k, n).wait_recv()
            own = row_ds(c)
            stored = slot * micro + m
            squares = jnp.zeros((rows, 1), jnp.float32)
            inner = jnp.zeros((rows, 1), jnp.float32)
            kept = []
            for n in range(blocks):
                cut = slice(n * quarter, (n + 1) * quarter)
                back = psend[item, own, cut].astype(jnp.float32)
                for k in range(1, tensors):
                    back += rbuf[item, k - 1, :, cut].astype(jnp.float32)
                scaled = g_ref[slot, :, cut] * back
                hidden = hbuf[stored, own, cut].astype(jnp.float32)
                squares += jnp.sum(hidden * hidden, axis=-1, keepdims=True)
                inner += jnp.sum(hidden * scaled, axis=-1, keepdims=True)
                kept.append(scaled)
            inverse_rms = lax.rsqrt(squares * (1.0 / width) + EPSILON)
            factor = inverse_rms * inverse_rms * inverse_rms * (inner * (1.0 / width))
            for n in range(blocks):
                cut = slice(n * quarter, (n + 1) * quarter)
                dnext[item, :, cut] = (
                    dbuf[item, own, cut].astype(jnp.float32)
                    + inverse_rms * kept[n]
                    - factor * hbuf[stored, own, cut].astype(jnp.float32)
                ).astype(jnp.bfloat16)
            b_along(item, target_item).start()

        return carry

    lax.fori_loop(0, items, b_step, 0)

    @pl.when(p == 0)
    def _():
        for m in range(micro):
            for k in range(1, tensors):
                opening(x_ref, hbuf, m, k).wait_send()

    @pl.when(p == pipes - 1)
    def _():
        for m in range(micro):
            for k in range(1, tensors):
                opening(cot_ref, dbuf, m, k).wait_send()

    def ending(item, carry):
        f_slot = item // micro
        b_slot = slots - 1 - item // micro
        m = lax.rem(item, micro)
        f_layer = f_slot * pipes + p
        b_layer = b_slot * pipes + p

        @pl.when(f_layer > 0)
        def _():
            for part in range(3):
                spread(f_slice, item, part, fx_send, fx_recv).wait_send()

        @pl.when(f_layer < layers - 1)
        def _():
            f_along(item, item).wait_send()

        @pl.when(b_layer < layers - 1)
        def _():
            for part in range(3):
                spread(b_slice, item, part, bx_send, bx_recv).wait_send()

        @pl.when(b_layer > 0)
        def _():
            b_along(item, item).wait_send()
            for n in range(blocks):
                for k in range(1, tensors):
                    reduce_copy(item, k, n).wait_send()

        to_own(hbuf, h_out, item, f_slot, m, 0).wait()
        to_own(dbuf, d_out, item, b_slot, m, 1).wait()
        for k in range(1, dps):
            to_dp(hbuf, h_out, item, f_slot, m, 0, k).wait()
            to_dp(dbuf, d_out, item, b_slot, m, 1, k).wait()
        return carry

    lax.fori_loop(0, items, ending, 0)


def chain(inputs, weights, norm_gains, cotangent):
    micro, rows, width = inputs.shape
    slots = weights.shape[0]
    quarter = weights.shape[3]
    pipes = lax.axis_size("pipe")
    tensors = lax.axis_size("tensor")
    dps = lax.axis_size("dp")
    items = slots * micro
    group = tensors * rows
    blocks = width // quarter
    dims = (micro, slots, rows, width, quarter, pipes, tensors, dps)
    vmem = pl.BlockSpec(memory_space=pltpu.VMEM)
    hbm = pl.BlockSpec(memory_space=pl.ANY)
    dma = pltpu.SemaphoreType.DMA
    out = jax.ShapeDtypeStruct((slots, dps, micro, group, width), jnp.bfloat16)
    return pl.pallas_call(
        functools.partial(chain_kernel, dims),
        out_shape=(out, out),
        in_specs=[vmem, hbm, vmem, vmem],
        out_specs=(hbm, hbm),
        scratch_shapes=[
            pltpu.VMEM((slots, width, quarter), jnp.bfloat16),
            pltpu.VMEM((items, group, width), jnp.bfloat16),
            pltpu.VMEM((items, group, width), jnp.bfloat16),
            pltpu.VMEM((group, quarter), jnp.float32),
            pltpu.VMEM((items, group, quarter), jnp.bfloat16),
            pltpu.VMEM((items, group, width), jnp.bfloat16),
            pltpu.VMEM((items, tensors - 1, rows, width), jnp.bfloat16),
            pltpu.VMEM((items, rows, width), jnp.bfloat16),
            dma((slots,)),
            dma((micro,)),
            dma((micro, tensors - 1)),
            dma((micro, tensors - 1)),
            dma((items,)),
            dma((items,)),
            dma((items, 3)),
            dma((items, 3)),
            dma((items,)),
            dma((items,)),
            dma((items, 3)),
            dma((items, 3)),
            dma((items, tensors - 1, blocks)),
            dma((items, tensors - 1, blocks)),
            dma((2, items, dps - 1)),
            dma((2, items, dps - 1)),
            dma((2, items)),
        ],
        compiler_params=pltpu.CompilerParams(
            collective_id=0, has_side_effects=True, vmem_limit_bytes=56 * 1024 * 1024
        ),
        name="chain",
    )(inputs, weights, norm_gains, cotangent)


def body(inputs, weights, norm_gains, cotangent):
    micro, rows, width = inputs.shape
    slots = weights.shape[0]
    quarter = weights.shape[3]
    tensors = lax.axis_size("tensor")
    dps = lax.axis_size("dp")
    own_rows = quarter // dps
    tokens = micro * rows * tensors * dps
    scale = 1.0 / tokens
    h_all, d_all = chain(inputs, weights, norm_gains, cotangent)
    base = (lax.axis_index("tensor") * dps + lax.axis_index("dp")) * own_rows
    h_all = h_all.reshape(slots, tokens, width)
    d_all = d_all.reshape(slots, tokens, width)
    wide = h_all.astype(jnp.float32)
    inverse_rms = lax.rsqrt(jnp.mean(wide * wide, axis=-1, keepdims=True) + EPSILON)
    normed = (wide * inverse_rms * norm_gains).astype(jnp.bfloat16)

    def factor(block):
        parts = []
        for s in range(slots):
            columns = lax.dynamic_slice_in_dim(block[s], base, own_rows, 1)
            gram = lax.dot_general(
                columns, block[s], (((0,), (0,)), ((), ())), preferred_element_type=jnp.float32
            )
            parts.append((gram * scale).astype(jnp.bfloat16))
        return jnp.stack(parts, 1)[:, :, None, :]

    return factor(normed), factor(d_all)


def solution(mesh):
    in_specs = (
        P(None, ("tensor", "dp"), None),
        P(None, "pipe", None, "tensor"),
        P(None, "pipe", None),
        P(None, ("tensor", "dp"), None),
    )
    out_specs = (P(("tensor", "dp"), None, "pipe", None), P(("tensor", "dp"), None, "pipe", None))
    return jax.shard_map(body, mesh=mesh, in_specs=in_specs, out_specs=out_specs, check_vma=False)
```

```python
import functools

import jax
import jax.numpy as jnp
from jax import lax
from jax.experimental import pallas as pl
from jax.experimental.pallas import tpu as pltpu
from jax.sharding import PartitionSpec as P

EPSILON = 1e-05


def peer_of(c, k):
    return lax.rem(c // 2 + k // 2, 2) * 2 + lax.rem(c + k, 2)


def chain_kernel(
    dims,
    x_ref,
    w_hbm,
    g_ref,
    cot_ref,
    h_out,
    d_out,
    w,
    hbuf,
    dcol,
    rms,
    acc,
    nxt,
    psend,
    rbuf,
    dnext,
    isend,
    irecv,
    w_sem,
    own_sem,
    in_send,
    in_recv,
    f1_send,
    f1_recv,
    fx_send,
    fx_recv,
    b1_send,
    b1_recv,
    rs_send,
    rs_recv,
    is_send,
    is_recv,
    dp_send,
    dp_recv,
    dg_send,
    dg_recv,
    loc_sem,
):
    micro, slots, rows, width, quarter, pipes, tensors, dps, cuts = dims
    items = slots * micro
    layers = slots * pipes
    group = tensors * rows
    part_rows = group // cuts
    p = lax.axis_index("pipe")
    c = lax.axis_index("tensor")
    d = lax.axis_index("dp")
    after = lax.rem(p + 1, pipes)
    before = lax.rem(p + pipes - 1, pipes)

    def where(pp, cc, dd):
        return {"pipe": pp, "tensor": cc, "dp": dd}

    def remote(src, dst, send, recv, target):
        return pltpu.make_async_remote_copy(
            src_ref=src,
            dst_ref=dst,
            send_sem=send,
            recv_sem=recv,
            device_id=target,
            device_id_type=pl.DeviceIdType.MESH,
        )

    w_copies = [
        pltpu.make_async_copy(w_hbm.at[s, 0], w.at[s], w_sem.at[s]) for s in range(slots)
    ]
    for copy in w_copies:
        copy.start()

    barrier = pltpu.get_barrier_semaphore()
    partners = [where(p, peer_of(c, k), d) for k in range(1, tensors)]
    partners += [where(after, c, d), where(before, c, d)]
    partners += [
        where(p, peer_of(c, k), lax.rem(d + e, dps)) for e in range(1, dps) for k in range(tensors)
    ]
    for partner in partners:
        pl.semaphore_signal(
            barrier, inc=1, device_id=partner, device_id_type=pl.DeviceIdType.MESH
        )
    pl.semaphore_wait(barrier, len(partners))

    def row_ds(cc):
        return pl.ds(pl.multiple_of(cc * rows, rows), rows)

    def col_ds(cc):
        return pl.ds(pl.multiple_of(cc * quarter, quarter), quarter)

    def opening(src, buf, m, k):
        whole = buf is hbuf
        return remote(
            src.at[m] if whole else src.at[m, :, col_ds(peer_of(c, k))],
            buf.at[m, row_ds(c)],
            in_send.at[m, k - 1],
            in_recv.at[m, k - 1],
            where(p, peer_of(c, k), d),
        )

    def opening_own(src, buf, m):
        whole = buf is hbuf
        return pltpu.make_async_copy(
            src.at[m] if whole else src.at[m, :, col_ds(c)], buf.at[m, row_ds(c)], own_sem.at[m]
        )

    def opening_all(src, buf):
        for m in range(micro):
            for k in range(1, tensors):
                opening(src, buf, m, k).start()
        for m in range(micro):
            opening_own(src, buf, m).start()

    def opening_wait(src, buf, m):
        opening_own(src, buf, m).wait()
        for k in range(1, tensors):
            opening(src, buf, m, k).wait_recv()

    @pl.when(p == 0)
    def _():
        opening_all(x_ref, hbuf)

    @pl.when(p == pipes - 1)
    def _():
        opening_all(cot_ref, dcol)

    def to_dp(item, slot, m, k):
        return remote(
            hbuf.at[item],
            h_out.at[slot, d, m],
            dp_send.at[item, k - 1],
            dp_recv.at[item, k - 1],
            where(p, c, lax.rem(d + k, dps)),
        )

    def to_own(item, slot, m):
        return pltpu.make_async_copy(hbuf.at[item], h_out.at[slot, d, m], loc_sem.at[0, item])

    def d_own(item, slot, m):
        return pltpu.make_async_copy(
            dcol.at[item], d_out.at[slot, d, m, :, col_ds(c)], loc_sem.at[1, item]
        )

    def d_share(item, slot, m, e, k):
        return remote(
            dcol.at[item],
            d_out.at[slot, d, m, :, col_ds(c)],
            dg_send.at[item, e, k],
            dg_recv.at[item, e, k],
            where(p, peer_of(c, k), lax.rem(d + e, dps)),
        )

    def d_shares(item, slot, m):
        return [
            d_share(item, slot, m, e, k)
            for e in range(dps - 1, -1, -1)
            for k in range(tensors - 1, -1, -1)
            if e or k
        ]

    def f_slice(item, cc, r):
        return hbuf.at[item, r * part_rows : (r + 1) * part_rows, col_ds(cc)]

    def f_along(item, target_item, r):
        return remote(
            nxt.at[item, r * part_rows : (r + 1) * part_rows],
            f_slice(target_item, c, r),
            f1_send.at[item, r],
            f1_recv.at[target_item, r],
            where(after, c, d),
        )

    def spread(item, part, r):
        owner = peer_of(c, 2) if part == 2 else c
        target = peer_of(c, 2) if part == 1 else peer_of(c, 1)
        ref = f_slice(item, owner, r)
        return remote(
            ref, ref, fx_send.at[item, part, r], fx_recv.at[item, part, r], where(p, target, d)
        )

    def f_step(item, carry):
        slot = item // micro
        m = lax.rem(item, micro)
        layer = slot * pipes + p
        target_item = item + micro * ((p + 1) // pipes)

        @pl.when(m == 0)
        def _():
            pltpu.make_async_copy(w_hbm.at[slot, 0], w.at[slot], w_sem.at[slot]).wait()

        @pl.when(layer == 0)
        def _():
            opening_wait(x_ref, hbuf, item)

        @pl.when(layer > 0)
        def _():
            for r in range(cuts):
                f_along(item, item, r).wait_recv()
                spread(item, 1, r).start()
                spread(item, 0, r).start()

        def piece(cc, first):
            part = hbuf[item, :, col_ds(cc)].astype(jnp.float32)
            scaled = (part * g_ref[slot, :, col_ds(cc)]).astype(jnp.bfloat16)
            product = jnp.dot(scaled, w[slot, col_ds(cc), :], preferred_element_type=jnp.float32)
            if first:
                acc[...] = product
            else:
                acc[...] += product
            return jnp.sum(part * part, axis=-1, keepdims=True)

        total = piece(c, True)

        @pl.when(layer > 0)
        def _():
            for r in range(cuts):
                spread(item, 0, r).wait_recv()

        total += piece(peer_of(c, 1), False)

        @pl.when(layer > 0)
        def _():
            for r in range(cuts):
                spread(item, 1, r).wait_recv()
                spread(item, 2, r).start()

        total += piece(peer_of(c, 2), False)

        @pl.when(layer > 0)
        def _():
            for r in range(cuts):
                spread(item, 2, r).wait_recv()

        total += piece(peer_of(c, 3), False)

        inverse_rms = lax.rsqrt(total * (1.0 / width) + EPSILON)
        rms[item] = jnp.broadcast_to(inverse_rms, (group, 128))

        @pl.when(layer < layers - 1)
        def _():
            product = (acc[...] * inverse_rms).astype(jnp.bfloat16).astype(jnp.float32)
            nxt[item] = (hbuf[item, :, col_ds(c)].astype(jnp.float32) + product).astype(
                jnp.bfloat16
            )
            for r in range(cuts):
                f_along(item, target_item, r).start()

        to_own(item, slot, m).start()
        for k in range(1, dps):
            to_dp(item, slot, m, k).start()
        return carry

    lax.fori_loop(0, items, f_step, 0)

    def b_along(item, target_item):
        return remote(
            dnext.at[item],
            dcol.at[target_item],
            b1_send.at[item],
            b1_recv.at[target_item],
            where(before, c, d),
        )

    def reduce_copy(item, k):
        return remote(
            psend.at[item, k],
            rbuf.at[item, k - 1],
            rs_send.at[item, k - 1],
            rs_recv.at[item, k - 1],
            where(p, peer_of(c, k), d),
        )

    def inner_copy(item, k):
        return remote(
            isend.at[item],
            irecv.at[item, k - 1],
            is_send.at[item, k - 1],
            is_recv.at[item, k - 1],
            where(p, peer_of(c, k), d),
        )

    def b_step(item, carry):
        slot = slots - 1 - item // micro
        m = lax.rem(item, micro)
        layer = slot * pipes + p
        target_item = item + micro * (1 - (p + pipes - 1) // pipes)
        stored = slot * micro + m

        @pl.when(layer == layers - 1)
        def _():
            opening_wait(cot_ref, dcol, item)

        @pl.when(layer < layers - 1)
        def _():
            b_along(item, item).wait_recv()

        @pl.when(layer == 0)
        def _():
            for share in d_shares(item, slot, m):
                share.start()

        d_own(item, slot, m).start()

        @pl.when(layer > 0)
        def _():
            columns = dcol[item]
            inner = jnp.zeros((group, 1), jnp.float32)
            for k in (3, 2, 1, 0):
                cc = peer_of(c, k)
                term = lax.dot_general(
                    columns,
                    w[slot, col_ds(cc), :],
                    (((1,), (1,)), ((), ())),
                    preferred_element_type=jnp.float32,
                ).astype(jnp.bfloat16)
                psend[item, k] = term
                if k:
                    reduce_copy(item, k).start()
                scaled = g_ref[slot, :, col_ds(cc)] * term.astype(jnp.float32)
                hidden = hbuf[stored, :, col_ds(cc)].astype(jnp.float32)
                inner += jnp.sum(hidden * scaled, axis=-1, keepdims=True)
            lanes = jnp.broadcast_to(inner, (group, 128))
            square = jnp.concatenate([lanes] * (128 // group), axis=0)
            isend[item] = jnp.transpose(square)[:8]
            for k in range(tensors - 1, 0, -1):
                inner_copy(item, k).start()

            for k in range(1, tensors):
                inner_copy(item, k).wait_recv()
            sums = isend[item]
            for k in range(1, tensors):
                sums += irecv[item, k - 1]
            inner_all = jnp.transpose(jnp.concatenate([sums] * 16, axis=0))[:group, :1]
            for k in (1, 2, 3):
                reduce_copy(item, k).wait_recv()
            back = psend[item, 0].astype(jnp.float32)
            for k in range(1, tensors):
                back += rbuf[item, k - 1].astype(jnp.float32)
            inverse_rms = rms[stored][:, :1]
            factor = inverse_rms * inverse_rms * inverse_rms * (inner_all * (1.0 / width))
            dnext[item] = (
                dcol[item].astype(jnp.float32)
                + inverse_rms * (g_ref[slot, :, col_ds(c)] * back)
                - factor * hbuf[stored, :, col_ds(c)].astype(jnp.float32)
            ).astype(jnp.bfloat16)
            b_along(item, target_item).start()

        @pl.when((layer > 0) & (m == micro - 1))
        def _():
            for q in range(micro):
                for share in d_shares(item - (micro - 1) + q, slot, q):
                    share.start()

        return carry

    lax.fori_loop(0, items, b_step, 0)

    @pl.when(p == 0)
    def _():
        for m in range(micro):
            for k in range(1, tensors):
                opening(x_ref, hbuf, m, k).wait_send()

    @pl.when(p == pipes - 1)
    def _():
        for m in range(micro):
            for k in range(1, tensors):
                opening(cot_ref, dcol, m, k).wait_send()

    def ending(item, carry):
        f_slot = item // micro
        b_slot = slots - 1 - item // micro
        m = lax.rem(item, micro)
        f_layer = f_slot * pipes + p
        b_layer = b_slot * pipes + p

        @pl.when(f_layer > 0)
        def _():
            for part in range(3):
                for r in range(cuts):
                    spread(item, part, r).wait_send()

        @pl.when(f_layer < layers - 1)
        def _():
            for r in range(cuts):
                f_along(item, item, r).wait_send()

        @pl.when(b_layer > 0)
        def _():
            b_along(item, item).wait_send()
            for k in range(1, tensors):
                reduce_copy(item, k).wait_send()
                inner_copy(item, k).wait_send()

        to_own(item, f_slot, m).wait()
        d_own(item, b_slot, m).wait()
        for k in range(1, dps):
            to_dp(item, f_slot, m, k).wait()
        for share in d_shares(item, b_slot, m):
            share.wait()
        return carry

    lax.fori_loop(0, items, ending, 0)


def chain(inputs, weights, norm_gains, cotangent):
    micro, rows, width = inputs.shape
    slots = weights.shape[0]
    quarter = weights.shape[3]
    pipes = lax.axis_size("pipe")
    tensors = lax.axis_size("tensor")
    dps = lax.axis_size("dp")
    items = slots * micro
    group = tensors * rows
    cuts = 4
    dims = (micro, slots, rows, width, quarter, pipes, tensors, dps, cuts)
    vmem = pl.BlockSpec(memory_space=pltpu.VMEM)
    hbm = pl.BlockSpec(memory_space=pl.ANY)
    dma = pltpu.SemaphoreType.DMA
    out = jax.ShapeDtypeStruct((slots, dps, micro, group, width), jnp.bfloat16)
    return pl.pallas_call(
        functools.partial(chain_kernel, dims),
        out_shape=(out, out),
        in_specs=[vmem, hbm, vmem, vmem],
        out_specs=(hbm, hbm),
        scratch_shapes=[
            pltpu.VMEM((slots, width, quarter), jnp.bfloat16),
            pltpu.VMEM((items, group, width), jnp.bfloat16),
            pltpu.VMEM((items, group, quarter), jnp.bfloat16),
            pltpu.VMEM((items, group, 128), jnp.float32),
            pltpu.VMEM((group, quarter), jnp.float32),
            pltpu.VMEM((items, group, quarter), jnp.bfloat16),
            pltpu.VMEM((items, tensors, group, quarter), jnp.bfloat16),
            pltpu.VMEM((items, tensors - 1, group, quarter), jnp.bfloat16),
            pltpu.VMEM((items, group, quarter), jnp.bfloat16),
            pltpu.VMEM((items, 8, 128), jnp.float32),
            pltpu.VMEM((items, tensors - 1, 8, 128), jnp.float32),
            dma((slots,)),
            dma((micro,)),
            dma((micro, tensors - 1)),
            dma((micro, tensors - 1)),
            dma((items, cuts)),
            dma((items, cuts)),
            dma((items, 3, cuts)),
            dma((items, 3, cuts)),
            dma((items,)),
            dma((items,)),
            dma((items, tensors - 1)),
            dma((items, tensors - 1)),
            dma((items, tensors - 1)),
            dma((items, tensors - 1)),
            dma((items, dps - 1)),
            dma((items, dps - 1)),
            dma((items, dps, tensors)),
            dma((items, dps, tensors)),
            dma((2, items)),
        ],
        compiler_params=pltpu.CompilerParams(
            collective_id=0, has_side_effects=True, vmem_limit_bytes=56 * 1024 * 1024
        ),
        name="chain",
    )(inputs, weights, norm_gains, cotangent)


def body(inputs, weights, norm_gains, cotangent):
    micro, rows, width = inputs.shape
    slots = weights.shape[0]
    quarter = weights.shape[3]
    tensors = lax.axis_size("tensor")
    dps = lax.axis_size("dp")
    own_rows = quarter // dps
    tokens = micro * rows * tensors * dps
    scale = 1.0 / tokens
    h_all, d_all = chain(inputs, weights, norm_gains, cotangent)
    base = (lax.axis_index("tensor") * dps + lax.axis_index("dp")) * own_rows
    h_all = h_all.reshape(slots, tokens, width)
    d_all = d_all.reshape(slots, tokens, width)
    wide = h_all.astype(jnp.float32)
    inverse_rms = lax.rsqrt(jnp.mean(wide * wide, axis=-1, keepdims=True) + EPSILON)
    normed = (wide * inverse_rms * norm_gains).astype(jnp.bfloat16)

    def factor(block):
        parts = []
        for s in range(slots):
            columns = lax.dynamic_slice_in_dim(block[s], base, own_rows, 1)
            gram = lax.dot_general(
                columns, block[s], (((0,), (0,)), ((), ())), preferred_element_type=jnp.float32
            )
            parts.append((gram * scale).astype(jnp.bfloat16))
        return jnp.stack(parts, 1)[:, :, None, :]

    return factor(normed), factor(d_all)


def solution(mesh):
    in_specs = (
        P(None, ("tensor", "dp"), None),
        P(None, "pipe", None, "tensor"),
        P(None, "pipe", None),
        P(None, ("tensor", "dp"), None),
    )
    out_specs = (P(("tensor", "dp"), None, "pipe", None), P(("tensor", "dp"), None, "pipe", None))
    return jax.shard_map(body, mesh=mesh, in_specs=in_specs, out_specs=out_specs, check_vma=False)
```

```python
import functools

import jax
import jax.numpy as jnp
from jax import lax
from jax.experimental import pallas as pl
from jax.experimental.pallas import tpu as pltpu
from jax.sharding import PartitionSpec as P

EPSILON = 1e-05


def peer_of(c, k):
    return lax.rem(c // 2 + k // 2, 2) * 2 + lax.rem(c + k, 2)


def chain_kernel(
    dims,
    x_ref,
    w_hbm,
    g_ref,
    cot_ref,
    h_out,
    d_out,
    w,
    hbuf,
    dcol,
    rms,
    acc,
    nxt,
    psend,
    rbuf,
    dnext,
    isend,
    irecv,
    w_sem,
    own_sem,
    in_send,
    in_recv,
    f1_send,
    f1_recv,
    fx_send,
    fx_recv,
    b1_send,
    b1_recv,
    rs_send,
    rs_recv,
    is_send,
    is_recv,
    dp_send,
    dp_recv,
    dg_send,
    dg_recv,
    loc_sem,
):
    micro, slots, rows, width, quarter, pipes, tensors, dps, cuts = dims
    items = slots * micro
    layers = slots * pipes
    group = tensors * rows
    part_rows = group // cuts
    p = lax.axis_index("pipe")
    c = lax.axis_index("tensor")
    d = lax.axis_index("dp")
    after = lax.rem(p + 1, pipes)
    before = lax.rem(p + pipes - 1, pipes)

    def where(pp, cc, dd):
        return {"pipe": pp, "tensor": cc, "dp": dd}

    def remote(src, dst, send, recv, target):
        return pltpu.make_async_remote_copy(
            src_ref=src,
            dst_ref=dst,
            send_sem=send,
            recv_sem=recv,
            device_id=target,
            device_id_type=pl.DeviceIdType.MESH,
        )

    w_copies = [
        pltpu.make_async_copy(w_hbm.at[s, 0], w.at[s], w_sem.at[s]) for s in range(slots)
    ]
    for copy in w_copies:
        copy.start()

    barrier = pltpu.get_barrier_semaphore()
    partners = [where(p, peer_of(c, k), d) for k in range(1, tensors)]
    partners += [where(after, c, d), where(before, c, d)]
    partners += [
        where(p, peer_of(c, k), lax.rem(d + e, dps)) for e in range(1, dps) for k in range(tensors)
    ]
    for partner in partners:
        pl.semaphore_signal(
            barrier, inc=1, device_id=partner, device_id_type=pl.DeviceIdType.MESH
        )
    pl.semaphore_wait(barrier, len(partners))

    def row_ds(cc):
        return pl.ds(pl.multiple_of(cc * rows, rows), rows)

    def col_ds(cc):
        return pl.ds(pl.multiple_of(cc * quarter, quarter), quarter)

    def opening(src, buf, m, k):
        whole = buf is hbuf
        return remote(
            src.at[m] if whole else src.at[m, :, col_ds(peer_of(c, k))],
            buf.at[m, row_ds(c)],
            in_send.at[m, k - 1],
            in_recv.at[m, k - 1],
            where(p, peer_of(c, k), d),
        )

    def opening_own(src, buf, m):
        whole = buf is hbuf
        return pltpu.make_async_copy(
            src.at[m] if whole else src.at[m, :, col_ds(c)], buf.at[m, row_ds(c)], own_sem.at[m]
        )

    def opening_all(src, buf):
        for m in range(micro):
            for k in range(1, tensors):
                opening(src, buf, m, k).start()
        for m in range(micro):
            opening_own(src, buf, m).start()

    def opening_wait(src, buf, m):
        opening_own(src, buf, m).wait()
        for k in range(1, tensors):
            opening(src, buf, m, k).wait_recv()

    @pl.when(p == 0)
    def _():
        opening_all(x_ref, hbuf)

    @pl.when(p == pipes - 1)
    def _():
        opening_all(cot_ref, dcol)

    def to_dp(item, slot, m, k):
        return remote(
            hbuf.at[item],
            h_out.at[slot, d, m],
            dp_send.at[item, k - 1],
            dp_recv.at[item, k - 1],
            where(p, c, lax.rem(d + k, dps)),
        )

    def to_own(item, slot, m):
        return pltpu.make_async_copy(hbuf.at[item], h_out.at[slot, d, m], loc_sem.at[0, item])

    def d_own(item, slot, m):
        return pltpu.make_async_copy(
            dcol.at[item], d_out.at[slot, d, m, :, col_ds(c)], loc_sem.at[1, item]
        )

    def d_share(item, slot, m, e, k):
        return remote(
            dcol.at[item],
            d_out.at[slot, d, m, :, col_ds(c)],
            dg_send.at[item, e, k],
            dg_recv.at[item, e, k],
            where(p, peer_of(c, k), lax.rem(d + e, dps)),
        )

    def d_shares(item, slot, m):
        return [
            d_share(item, slot, m, e, k)
            for e in range(dps - 1, -1, -1)
            for k in range(tensors - 1, -1, -1)
            if e or k
        ]

    def f_slice(item, cc, r):
        return hbuf.at[item, r * part_rows : (r + 1) * part_rows, col_ds(cc)]

    def f_along(item, target_item, r):
        return remote(
            nxt.at[item, r * part_rows : (r + 1) * part_rows],
            f_slice(target_item, c, r),
            f1_send.at[item, r],
            f1_recv.at[target_item, r],
            where(after, c, d),
        )

    def spread(item, part, r):
        owner = peer_of(c, 2) if part == 2 else c
        target = peer_of(c, 2) if part == 1 else peer_of(c, 1)
        ref = f_slice(item, owner, r)
        return remote(
            ref, ref, fx_send.at[item, part, r], fx_recv.at[item, part, r], where(p, target, d)
        )

    def f_step(item, carry):
        slot = item // micro
        m = lax.rem(item, micro)
        layer = slot * pipes + p
        target_item = item + micro * ((p + 1) // pipes)

        @pl.when(m == 0)
        def _():
            pltpu.make_async_copy(w_hbm.at[slot, 0], w.at[slot], w_sem.at[slot]).wait()

        @pl.when(layer == 0)
        def _():
            opening_wait(x_ref, hbuf, item)

        @pl.when(layer > 0)
        def _():
            for r in range(cuts):
                f_along(item, item, r).wait_recv()
                spread(item, 1, r).start()
                spread(item, 0, r).start()

        def piece(cc, first):
            part = hbuf[item, :, col_ds(cc)].astype(jnp.float32)
            scaled = (part * g_ref[slot, :, col_ds(cc)]).astype(jnp.bfloat16)
            product = jnp.dot(scaled, w[slot, col_ds(cc), :], preferred_element_type=jnp.float32)
            if first:
                acc[...] = product
            else:
                acc[...] += product
            return jnp.sum(part * part, axis=-1, keepdims=True)

        total = piece(c, True)

        @pl.when(layer > 0)
        def _():
            for r in range(cuts):
                spread(item, 0, r).wait_recv()

        total += piece(peer_of(c, 1), False)

        @pl.when(layer > 0)
        def _():
            for r in range(cuts):
                spread(item, 1, r).wait_recv()
                spread(item, 2, r).start()

        total += piece(peer_of(c, 2), False)

        @pl.when(layer > 0)
        def _():
            for r in range(cuts):
                spread(item, 2, r).wait_recv()

        total += piece(peer_of(c, 3), False)

        inverse_rms = lax.rsqrt(total * (1.0 / width) + EPSILON)
        rms[item] = jnp.broadcast_to(inverse_rms, (group, 128))

        @pl.when(layer < layers - 1)
        def _():
            product = (acc[...] * inverse_rms).astype(jnp.bfloat16).astype(jnp.float32)
            nxt[item] = (hbuf[item, :, col_ds(c)].astype(jnp.float32) + product).astype(
                jnp.bfloat16
            )
            for r in range(cuts):
                f_along(item, target_item, r).start()

        to_own(item, slot, m).start()
        for k in range(1, dps):
            to_dp(item, slot, m, k).start()
        return carry

    lax.fori_loop(0, items, f_step, 0)

    def b_along(item, target_item):
        return remote(
            dnext.at[item],
            dcol.at[target_item],
            b1_send.at[item],
            b1_recv.at[target_item],
            where(before, c, d),
        )

    def reduce_copy(item, k):
        return remote(
            psend.at[item, k],
            rbuf.at[item, k - 1],
            rs_send.at[item, k - 1],
            rs_recv.at[item, k - 1],
            where(p, peer_of(c, k), d),
        )

    def inner_copy(item, k):
        return remote(
            isend.at[item],
            irecv.at[item, k - 1],
            is_send.at[item, k - 1],
            is_recv.at[item, k - 1],
            where(p, peer_of(c, k), d),
        )

    def b_step(item, carry):
        slot = slots - 1 - item // micro
        m = lax.rem(item, micro)
        layer = slot * pipes + p
        target_item = item + micro * (1 - (p + pipes - 1) // pipes)
        stored = slot * micro + m

        @pl.when(layer == layers - 1)
        def _():
            opening_wait(cot_ref, dcol, item)

        @pl.when(layer < layers - 1)
        def _():
            b_along(item, item).wait_recv()

        @pl.when(layer == 0)
        def _():
            for share in d_shares(item, slot, m):
                share.start()

        d_own(item, slot, m).start()

        @pl.when(layer > 0)
        def _():
            columns = dcol[item]
            inner = jnp.zeros((group, 1), jnp.float32)
            for k in (3, 2, 1, 0):
                cc = peer_of(c, k)
                term = lax.dot_general(
                    columns,
                    w[slot, col_ds(cc), :],
                    (((1,), (1,)), ((), ())),
                    preferred_element_type=jnp.float32,
                ).astype(jnp.bfloat16)
                psend[item, k] = term
                if k:
                    reduce_copy(item, k).start()
                scaled = g_ref[slot, :, col_ds(cc)] * term.astype(jnp.float32)
                hidden = hbuf[stored, :, col_ds(cc)].astype(jnp.float32)
                inner += jnp.sum(hidden * scaled, axis=-1, keepdims=True)
            lanes = jnp.broadcast_to(inner, (group, 128))
            square = jnp.concatenate([lanes] * (128 // group), axis=0)
            isend[item] = jnp.transpose(square)[:8]
            for k in range(tensors - 1, 0, -1):
                inner_copy(item, k).start()

            for k in range(1, tensors):
                inner_copy(item, k).wait_recv()
            sums = isend[item]
            for k in range(1, tensors):
                sums += irecv[item, k - 1]
            inner_all = jnp.transpose(jnp.concatenate([sums] * 16, axis=0))[:group, :1]
            for k in (1, 2, 3):
                reduce_copy(item, k).wait_recv()
            back = psend[item, 0].astype(jnp.float32)
            for k in range(1, tensors):
                back += rbuf[item, k - 1].astype(jnp.float32)
            inverse_rms = rms[stored][:, :1]
            factor = inverse_rms * inverse_rms * inverse_rms * (inner_all * (1.0 / width))
            dnext[item] = (
                dcol[item].astype(jnp.float32)
                + inverse_rms * (g_ref[slot, :, col_ds(c)] * back)
                - factor * hbuf[stored, :, col_ds(c)].astype(jnp.float32)
            ).astype(jnp.bfloat16)
            b_along(item, target_item).start()

        @pl.when((layer > 0) & (m == micro - 1))
        def _():
            for q in range(micro):
                for share in d_shares(item - (micro - 1) + q, slot, q):
                    share.start()

        return carry

    lax.fori_loop(0, items, b_step, 0)

    @pl.when(p == 0)
    def _():
        for m in range(micro):
            for k in range(1, tensors):
                opening(x_ref, hbuf, m, k).wait_send()

    @pl.when(p == pipes - 1)
    def _():
        for m in range(micro):
            for k in range(1, tensors):
                opening(cot_ref, dcol, m, k).wait_send()

    def ending(item, carry):
        f_slot = item // micro
        b_slot = slots - 1 - item // micro
        m = lax.rem(item, micro)
        f_layer = f_slot * pipes + p
        b_layer = b_slot * pipes + p

        @pl.when(f_layer > 0)
        def _():
            for part in range(3):
                for r in range(cuts):
                    spread(item, part, r).wait_send()

        @pl.when(f_layer < layers - 1)
        def _():
            for r in range(cuts):
                f_along(item, item, r).wait_send()

        @pl.when(b_layer > 0)
        def _():
            b_along(item, item).wait_send()
            for k in range(1, tensors):
                reduce_copy(item, k).wait_send()
                inner_copy(item, k).wait_send()

        to_own(item, f_slot, m).wait()
        d_own(item, b_slot, m).wait()
        for k in range(1, dps):
            to_dp(item, f_slot, m, k).wait()
        for share in d_shares(item, b_slot, m):
            share.wait()
        return carry

    lax.fori_loop(0, items, ending, 0)


def chain(inputs, weights, norm_gains, cotangent):
    micro, rows, width = inputs.shape
    slots = weights.shape[0]
    quarter = weights.shape[3]
    pipes = lax.axis_size("pipe")
    tensors = lax.axis_size("tensor")
    dps = lax.axis_size("dp")
    items = slots * micro
    group = tensors * rows
    cuts = 4
    dims = (micro, slots, rows, width, quarter, pipes, tensors, dps, cuts)
    vmem = pl.BlockSpec(memory_space=pltpu.VMEM)
    hbm = pl.BlockSpec(memory_space=pl.ANY)
    dma = pltpu.SemaphoreType.DMA
    out = jax.ShapeDtypeStruct((slots, dps, micro, group, width), jnp.bfloat16)
    return pl.pallas_call(
        functools.partial(chain_kernel, dims),
        out_shape=(out, out),
        in_specs=[vmem, hbm, vmem, vmem],
        out_specs=(hbm, hbm),
        scratch_shapes=[
            pltpu.VMEM((slots, width, quarter), jnp.bfloat16),
            pltpu.VMEM((items, group, width), jnp.bfloat16),
            pltpu.VMEM((items, group, quarter), jnp.bfloat16),
            pltpu.VMEM((items, group, 128), jnp.float32),
            pltpu.VMEM((group, quarter), jnp.float32),
            pltpu.VMEM((items, group, quarter), jnp.bfloat16),
            pltpu.VMEM((items, tensors, group, quarter), jnp.bfloat16),
            pltpu.VMEM((items, tensors - 1, group, quarter), jnp.bfloat16),
            pltpu.VMEM((items, group, quarter), jnp.bfloat16),
            pltpu.VMEM((items, 8, 128), jnp.float32),
            pltpu.VMEM((items, tensors - 1, 8, 128), jnp.float32),
            dma((slots,)),
            dma((micro,)),
            dma((micro, tensors - 1)),
            dma((micro, tensors - 1)),
            dma((items, cuts)),
            dma((items, cuts)),
            dma((items, 3, cuts)),
            dma((items, 3, cuts)),
            dma((items,)),
            dma((items,)),
            dma((items, tensors - 1)),
            dma((items, tensors - 1)),
            dma((items, tensors - 1)),
            dma((items, tensors - 1)),
            dma((items, dps - 1)),
            dma((items, dps - 1)),
            dma((items, dps, tensors)),
            dma((items, dps, tensors)),
            dma((2, items)),
        ],
        compiler_params=pltpu.CompilerParams(
            collective_id=0, has_side_effects=True, vmem_limit_bytes=56 * 1024 * 1024
        ),
        name="chain",
    )(inputs, weights, norm_gains, cotangent)


def gram_kernel(base_rows, scale, normalized, x_ref, g_ref, out_ref, full, mixed):
    slots, tokens, width = x_ref.shape
    block = out_ref.shape[0]
    step = pl.program_id(0)

    if normalized:

        @pl.when(step == 0)
        def _():
            for s in range(slots):
                for t in range(0, tokens, 32):
                    wide = x_ref[s, t : t + 32].astype(jnp.float32)
                    mean = jnp.mean(wide * wide, axis=-1, keepdims=True)
                    inverse_rms = lax.rsqrt(mean + EPSILON)
                    full[s, t : t + 32] = (wide * inverse_rms * g_ref[s]).astype(jnp.bfloat16)

    source = full if normalized else x_ref
    own = (lax.axis_index("tensor") * lax.axis_size("dp") + lax.axis_index("dp")) * base_rows
    start = pl.multiple_of(own + step * block, block)
    columns = [source[s, :, pl.ds(start, block)] for s in range(slots)]
    span = 512
    for n in range(width // span):
        cut = slice(n * span, (n + 1) * span)
        for s in range(slots):
            gram = lax.dot_general(
                columns[s],
                source[s, :, cut],
                (((0,), (0,)), ((), ())),
                preferred_element_type=jnp.float32,
            )
            for q in range(span // 128):
                mixed[q, pl.ds(s, block, slots), :] = gram[:, q * 128 : (q + 1) * 128] * scale
        for q in range(span // 128):
            lane = slice(n * span + q * 128, n * span + (q + 1) * 128)
            out_ref[:, :, lane] = mixed[q].astype(jnp.bfloat16).reshape(block, slots, 128)


def gram_call(block, gains, own_rows, normalized):
    slots, tokens, width = block.shape
    tile = min(128, own_rows)
    out = pl.pallas_call(
        functools.partial(gram_kernel, own_rows, 1.0 / tokens, normalized),
        grid=(own_rows // tile,),
        out_shape=jax.ShapeDtypeStruct((own_rows, slots, width), jnp.bfloat16),
        in_specs=[
            pl.BlockSpec(block.shape, lambda i: (0, 0, 0), pipeline_mode=pl.Buffered(1)),
            pl.BlockSpec(gains.shape, lambda i: (0, 0, 0), pipeline_mode=pl.Buffered(1)),
        ],
        out_specs=pl.BlockSpec((tile, slots, width), lambda i: (i, 0, 0)),
        scratch_shapes=[
            pltpu.VMEM((slots, tokens, width) if normalized else (slots, 8, 128), jnp.bfloat16),
            pltpu.VMEM((4, tile * slots, 128), jnp.float32),
        ],
        compiler_params=pltpu.CompilerParams(vmem_limit_bytes=min(62 << 20, (32 << 20) + 8 * block.size)),
        name="gram",
    )(block, gains)
    return out.reshape(own_rows, slots, 1, width)


def body(inputs, weights, norm_gains, cotangent):
    micro, rows, width = inputs.shape
    slots = weights.shape[0]
    quarter = weights.shape[3]
    tensors = lax.axis_size("tensor")
    dps = lax.axis_size("dp")
    own_rows = quarter // dps
    tokens = micro * rows * tensors * dps
    h_all, d_all = chain(inputs, weights, norm_gains, cotangent)
    h_all = h_all.reshape(slots, tokens, width)
    d_all = d_all.reshape(slots, tokens, width)
    act = gram_call(h_all, norm_gains, own_rows, True)
    return act, gram_call(d_all, norm_gains, own_rows, False)


def solution(mesh):
    in_specs = (
        P(None, ("tensor", "dp"), None),
        P(None, "pipe", None, "tensor"),
        P(None, "pipe", None),
        P(None, ("tensor", "dp"), None),
    )
    out_specs = (P(("tensor", "dp"), None, "pipe", None), P(("tensor", "dp"), None, "pipe", None))
    return jax.shard_map(body, mesh=mesh, in_specs=in_specs, out_specs=out_specs, check_vma=False)
```
